768 devices in a mesh: pipe: 12 (over z), ep: 64 (over y, x, core).
Axes of the slice: x: 4, y: 8, z: 12, core: 2. Of those that a mesh axis runs over, the one named last changes fastest.
Arguments:
- activations: bfloat16 [12, 192, 7168], P('pipe', 'ep'), may hold values from -6 to 6
- cotangent: bfloat16 [12, 192, 7168], P('pipe', 'ep'), may hold values from -6 to 6
- forward_experts: int32 [12, 192, 4], P('pipe', 'ep'), may hold values from 0 to 7, all different within a row; in each aligned block of 3 rows (0 to 2, 3 to 5, ..., all dimensions but the last counted through in order) at most 2 rows name the same one
- forward_weights: float32 [12, 192, 4], P('pipe', 'ep'), may hold values from 0.2 to 1
- backward_experts: int32 [12, 192, 4], P('pipe', 'ep'), may hold values from 0 to 7, all different within a row; in each aligned block of 3 rows (0 to 2, 3 to 5, ..., all dimensions but the last counted through in order) at most 2 rows name the same one
- backward_weights: float32 [12, 192, 4], P('pipe', 'ep'), may hold values from 0.2 to 1
- gate_weight: bfloat16 [7168, 16384], P(None, 'ep'), may hold values from -0.0625 to 0.0625
- up_weight: bfloat16 [7168, 16384], P(None, 'ep'), may hold values from -0.0625 to 0.0625
- down_weight: bfloat16 [16384, 7168], P('ep'), may hold values from -0.125 to 0.125
- saved_gate: bfloat16 [12, 128, 16384], P('pipe', None, 'ep'), may hold values from -6 to 6
- saved_up: bfloat16 [12, 128, 16384], P('pipe', None, 'ep'), may hold values from -6 to 6
Outputs:
- input_handoff: bfloat16 [12, 192, 7168], P('pipe', 'ep')
- grad_handoff: bfloat16 [12, 192, 7168], P('pipe', 'ep')
The draws below stay inside these ranges and needn't reach their ends.
Inputs may be any that keep to these rules, and one draw needn't show every extreme that they name: `forward_experts`: each token names 4 different experts. Within the 3 tokens of one device at one section, no expert is named more than 2 times, and some device names some expert exactly 2 times. `backward_experts`: each token names 4 different experts. Within the 3 tokens of one device at one section, no expert is named more than 2 times, and some device names some expert exactly 2 times.
All inputs are finite; a program needn't handle non-finite values.
Results may differ from the reference program's by a relative error of at most 0.0058.
Values may be sent and summed in bfloat16 or wider, within the bound.
A program may use at most 128 MiB of HBM per device.

```python
import math
import jax
import jax.numpy as jnp
import numpy as np
from jax import lax

D = 7168
FF = 2048
EXPERTS = 8
TOP = 4
TOK_DEV = 3
SHARDS = 8
FF_DEV = 256
CAP = 2
TOKENS = 192
SLOTS = 128
N_PIPE = 12
N_EP = 64


def block_levels(stream_key, shape, split, smallest, largest):
    gain = 1.0
    for axis_at, parts in split:
        heights = jax.random.uniform(jax.random.fold_in(jax.random.fold_in(stream_key, 6), axis_at), (parts,), jnp.float32, smallest / len(split), largest / len(split))
        gain = gain * jnp.repeat(jnp.exp(heights), shape[axis_at] // parts).reshape((-1,) + (1,) * (len(shape) - 1 - axis_at))
    return gain


def assign_block(stream_key, own, number, rows, number_of, top, reach, skew):
    order = jax.random.permutation(stream_key, number_of)
    packed, common = portions_of(number_of, rows * top, reach, skew, True), portions_of(number_of, rows * top, reach, skew, False)
    places = jnp.arange(number_of)

    def named(tallies, rotation):
        used = int((tallies > 0).sum())
        fixed = max(1, used // 4)
        shifted = fixed + (places - fixed + rotation * (used - fixed)) % max(1, number_of - fixed)
        return jnp.zeros((number_of,), jnp.int32).at[order[jnp.where(places < fixed, places, shifted)]].set(jnp.asarray(tallies, jnp.int32))

    tallies = jnp.where(number % 4 == 0, named(packed, number // 4), named(common, number - number // 4 - 1))
    mixed = jax.random.permutation(jax.random.fold_in(own, 3), number_of)
    giver, taker = mixed[0:number_of // 2 * 2:2], mixed[1:number_of // 2 * 2:2]
    margin = jnp.minimum(tallies[giver] - 1, reach - tallies[taker]) // 2
    margin = jnp.where((giver == order[0]) | (taker == order[0]) | (tallies[taker] == 0), 0, jnp.maximum(margin, 0))
    shifted = jax.random.randint(jax.random.fold_in(own, 4), (number_of // 2,), 0, 1 << 20) % (margin + 1)
    tallies = tallies.at[giver].add(-shifted).at[taker].add(shifted)
    items = jnp.searchsorted(jnp.cumsum(tallies), jnp.arange(rows * top), side="right").astype(jnp.int32)
    table = items.reshape(top, rows).T
    table = table[jax.random.permutation(jax.random.fold_in(own, 1), rows)]
    rotation = jax.random.randint(jax.random.fold_in(own, 2), (rows, 1), 0, top)
    return jnp.take_along_axis(table, (jnp.arange(top)[None, :] + rotation) % top, axis=1)


def portions_of(number_of, total, limit, slope, full):
    loads = [(1 << 20) // math.isqrt(standing ** slope) + 1 for standing in range(1, number_of + 1)]
    largest = limit if full else min(limit, max(-(-total // number_of), total * loads[0] // sum(loads)))
    least = 1 if total - largest >= number_of - 1 else 0
    counts, surplus = [largest] + [least] * (number_of - 1), total - largest - least * (number_of - 1)
    while surplus > 0:
        movable = [i for i in range(1, number_of) if counts[i] < largest] or [i for i in range(1, number_of) if counts[i] < limit]
        mass, left = sum([loads[i] for i in movable]), surplus
        for i in movable:
            addition = min(limit - counts[i], max(1, left * loads[i] // mass), surplus)
            counts[i] = counts[i] + addition
            surplus = surplus - addition
    return np.array(counts)


def gaussian(own_key, dims, scale, most, split=(), kind=jnp.bfloat16):
    values = jax.random.normal(own_key, dims, jnp.float32) * scale
    if len(split) > 0:
        values = block_levels(own_key, dims, split, -0.22, 0.18) * values
    return jnp.clip(values, min=-most, max=most).astype(kind)


def setup_inputs(seed: int = 0) -> dict:
    key_list = jax.random.split(jax.random.key(seed), 12)
    activations = gaussian(key_list[0], (N_PIPE, TOKENS, D), 1.0, 6.0, ((0, 12), (1, 64)))
    cotangent = gaussian(key_list[1], (N_PIPE, TOKENS, D), 1.0, 6.0, ((0, 12), (1, 64)))
    forward_experts_keys = jax.random.split(jax.random.fold_in(key_list[2], 1), N_PIPE * TOKENS // TOK_DEV)
    forward_experts_turns = jax.random.permutation(jax.random.fold_in(key_list[2], 3), N_PIPE * TOKENS // TOK_DEV)
    forward_experts = jax.vmap(lambda own, number: assign_block(jax.random.fold_in(key_list[2], 2), own, number, TOK_DEV, EXPERTS, TOP, CAP, 2))(forward_experts_keys, forward_experts_turns).reshape((N_PIPE, TOKENS, TOP))
    forward_weights = jnp.clip(0.2 + 0.8 * jax.random.uniform(key_list[3], (N_PIPE, TOKENS, TOP), jnp.float32) ** block_levels(key_list[3], (N_PIPE, TOKENS, TOP), ((0, 12), (1, 64)), -0.2, 0.2), 0.2, 1.0)
    backward_experts_keys = jax.random.split(jax.random.fold_in(key_list[4], 1), N_PIPE * TOKENS // TOK_DEV)
    backward_experts_turns = jax.random.permutation(jax.random.fold_in(key_list[4], 3), N_PIPE * TOKENS // TOK_DEV)
    backward_experts = jax.vmap(lambda own, number: assign_block(jax.random.fold_in(key_list[4], 2), own, number, TOK_DEV, EXPERTS, TOP, CAP, 2))(backward_experts_keys, backward_experts_turns).reshape((N_PIPE, TOKENS, TOP))
    backward_weights = jnp.clip(0.2 + 0.8 * jax.random.uniform(key_list[5], (N_PIPE, TOKENS, TOP), jnp.float32) ** block_levels(key_list[5], (N_PIPE, TOKENS, TOP), ((0, 12), (1, 64)), -0.2, 0.2), 0.2, 1.0)
    gate_weight = gaussian(key_list[6], (D, EXPERTS * FF), D ** -0.5, 0.0625, ((1, 64),))
    up_weight = gaussian(key_list[7], (D, EXPERTS * FF), D ** -0.5, 0.0625, ((1, 64),))
    down_weight = gaussian(key_list[8], (EXPERTS * FF, D), FF ** -0.5, 0.125, ((0, 64),))
    saved_gate = gaussian(key_list[9], (N_PIPE, SLOTS, EXPERTS * FF), 1.5, 6.0, ((0, 12), (2, 64)))
    saved_up = gaussian(key_list[10], (N_PIPE, SLOTS, EXPERTS * FF), 1.0, 6.0, ((0, 12), (2, 64)))
    return dict(activations=activations, cotangent=cotangent, forward_experts=forward_experts, forward_weights=forward_weights, backward_experts=backward_experts, backward_weights=backward_weights, gate_weight=gate_weight, up_weight=up_weight, down_weight=down_weight, saved_gate=saved_gate, saved_up=saved_up)


def slot_numbers(expert_ids):
    flat_ids = expert_ids.reshape(N_EP, TOK_DEV * TOP)
    onehot = (flat_ids[:, :, None] == jnp.arange(EXPERTS, dtype=jnp.int32)[None, None, :]).astype(jnp.int32)
    before = jnp.cumsum(onehot, axis=1) - onehot
    return jnp.sum(before * onehot, axis=2).reshape(TOKENS, TOP).astype(jnp.int32)


def rounded(values):
    narrow = values.astype(jnp.bfloat16)
    return lax.optimization_barrier(narrow).astype(jnp.float32)


def forward_section(activations, expert_ids, route_weights, gate_weight, up_weight, down_weight):
    running = activations.astype(jnp.float32)
    for expert in range(EXPERTS):
        begin_unit = expert * FF
        end_unit = (expert + 1) * FF
        gate_pre = jnp.dot(activations, gate_weight[:, begin_unit:end_unit], preferred_element_type=jnp.float32)
        up_pre = jnp.dot(activations, up_weight[:, begin_unit:end_unit], preferred_element_type=jnp.float32)
        hidden = (jax.nn.silu(gate_pre) * up_pre).astype(jnp.bfloat16)
        down_expert = down_weight[begin_unit:end_unit].astype(jnp.float32).reshape(SHARDS, FF_DEV, D)
        partials = jnp.einsum("tsk,skd->tsd", hidden.astype(jnp.float32).reshape(TOKENS, SHARDS, FF_DEV), down_expert)
        expert_out = jnp.sum(rounded(partials), axis=1)
        share = jnp.sum(jnp.where(expert_ids == expert, route_weights, jnp.zeros_like(route_weights)), axis=1)
        running = running + share[:, None] * expert_out
    return running.astype(jnp.bfloat16)


def backward_section(cotangent, expert_ids, route_weights, gate_weight, up_weight, down_weight, saved_gate, saved_up):
    source_row = (jnp.arange(TOKENS, dtype=jnp.int32) // TOK_DEV)[:, None] * CAP + slot_numbers(expert_ids)
    grad_in = cotangent.astype(jnp.float32)
    running = grad_in
    scaled_all = [(route_weights[:, chosen:chosen + 1] * grad_in).astype(jnp.bfloat16) for chosen in range(TOP)]
    gate_all = [jnp.take(saved_gate, source_row[:, chosen], axis=0) for chosen in range(TOP)]
    up_all = [jnp.take(saved_up, source_row[:, chosen], axis=0) for chosen in range(TOP)]
    for expert in range(EXPERTS):
        begin_unit = expert * FF
        end_unit = (expert + 1) * FF
        scaled = jnp.zeros((TOKENS, D), jnp.bfloat16)
        gate_rows = jnp.zeros((TOKENS, FF), jnp.bfloat16)
        up_rows = jnp.zeros((TOKENS, FF), jnp.bfloat16)
        for chosen in range(TOP):
            picked = expert_ids[:, chosen:chosen + 1] == expert
            scaled = jnp.where(picked, scaled_all[chosen], scaled)
            gate_rows = jnp.where(picked, gate_all[chosen][:, begin_unit:end_unit], gate_rows)
            up_rows = jnp.where(picked, up_all[chosen][:, begin_unit:end_unit], up_rows)
        grad_hidden = lax.dot_general(scaled, down_weight[begin_unit:end_unit], (((1,), (1,)), ((), ())), preferred_element_type=jnp.float32)
        gate_value = gate_rows.astype(jnp.float32)
        up_value = up_rows.astype(jnp.float32)
        sigmoid_gate = jax.nn.sigmoid(gate_value)
        gate_grad = (grad_hidden * up_value * sigmoid_gate * (1.0 + gate_value * (1.0 - sigmoid_gate))).astype(jnp.bfloat16)
        up_grad = (grad_hidden * (gate_value * sigmoid_gate)).astype(jnp.bfloat16)
        gate_expert = gate_weight[:, begin_unit:end_unit].astype(jnp.float32).reshape(D, SHARDS, FF_DEV)
        up_expert = up_weight[:, begin_unit:end_unit].astype(jnp.float32).reshape(D, SHARDS, FF_DEV)
        partials = jnp.einsum("tsk,dsk->tsd", gate_grad.astype(jnp.float32).reshape(TOKENS, SHARDS, FF_DEV), gate_expert)
        partials = partials + jnp.einsum("tsk,dsk->tsd", up_grad.astype(jnp.float32).reshape(TOKENS, SHARDS, FF_DEV), up_expert)
        contrib = jnp.sum(rounded(partials), axis=1)
        used = jnp.any(expert_ids == expert, axis=1)[:, None]
        running = running + jnp.where(used, contrib, jnp.zeros_like(contrib))
    return running.astype(jnp.bfloat16)


def reference(activations, cotangent, forward_experts, forward_weights, backward_experts, backward_weights, gate_weight, up_weight, down_weight, saved_gate, saved_up):
    layer_outs = []
    input_grads = []
    for section_index in range(N_PIPE):
        layer_outs.append(forward_section(activations[section_index], forward_experts[section_index], forward_weights[section_index], gate_weight, up_weight, down_weight))
        input_grads.append(backward_section(cotangent[section_index], backward_experts[section_index], backward_weights[section_index], gate_weight, up_weight, down_weight, saved_gate[section_index], saved_up[section_index]))
    blank_section = jnp.zeros((1, TOKENS, D), jnp.bfloat16)
    input_handoff = jnp.concatenate([blank_section, jnp.stack(layer_outs[:-1])], axis=0)
    grad_handoff = jnp.concatenate([jnp.stack(input_grads[1:]), blank_section], axis=0)
    return (input_handoff, grad_handoff)
```

```python
import functools

import jax
import jax.numpy as jnp
from jax import lax
from jax.experimental import pallas as pl
from jax.experimental.pallas import tpu as pltpu
from jax.sharding import PartitionSpec as P

EXPERTS = 8
TOP = 4
CAP = 2
TOK = 3
CORES = 2
RING = 4
CHUNKS = 4
MESH = pl.DeviceIdType.MESH
LAST = (((1,), (1,)), ((), ()))


def kernel(
    cuts,
    act_hbm,
    cot_hbm,
    fexp,
    fwt,
    bexp,
    bwt,
    wg_hbm,
    wu_hbm,
    wd_hbm,
    sg_hbm,
    su_hbm,
    out_f,
    out_b,
    tok,
    wg,
    wu,
    wd,
    sg,
    su,
    ysend,
    yrecv,
    rows,
    gacc,
    uacc,
    hacc,
    hid,
    ggrad,
    ugrad,
    psend,
    precv,
    pown,
    t2s,
    t2r,
    ts,
    tr,
    hs,
    hr,
    osend,
    in_sem,
    y_ss,
    y_rs,
    x_ss,
    x_rs,
    r_ss,
    r_rs,
    h_ss,
    h_rs,
    z_ss,
    z_rs,
):
    sections = lax.axis_size("pipe")
    section = lax.axis_index("pipe")
    place = lax.axis_index("ep")
    y = place // (RING * CORES)
    x = (place // CORES) % RING
    c = place % CORES
    width = tok.shape[2]
    wide = width // cuts
    half = wide // 2
    block = EXPERTS * CAP
    side = RING * block
    outs = (out_f, out_b)

    def at(yy, xx, cc):
        return (section, (yy * RING + xx) * CORES + cc)

    right = at(y, (x + 1) % RING, c)
    left = at(y, (x + RING - 1) % RING, c)
    partner = at(y, x, 1 - c)

    def expert_of(d):
        return at((y + EXPERTS - d) % EXPERTS, x, c)

    def source_of(d):
        return at((y + d) % EXPERTS, x, c)

    def cols(ch):
        return pl.ds(ch * wide, wide)

    def remote(src, dst, ss, rs, dev):
        return pltpu.make_async_remote_copy(
            src_ref=src, dst_ref=dst, send_sem=ss, recv_sem=rs, device_id=dev, device_id_type=MESH
        )

    loads = {}

    def load(name, src, dst, number):
        copy = pltpu.make_async_copy(src, dst, in_sem.at[number])
        copy.start()
        loads[name] = copy

    def need(name):
        copy = loads.pop(name, None)
        if copy is not None:
            copy.wait()

    load("act", act_hbm.at[0], tok.at[0], 0)
    load("cot", cot_hbm.at[0], tok.at[1], 1)
    load("wg", wg_hbm, wg, 2)
    load("wu", wu_hbm, wu, 3)
    load("wd", wd_hbm, wd, 4)
    load("sg", sg_hbm.at[0], sg, 5)
    load("su", su_hbm.at[0], su, 6)

    barrier = pltpu.get_barrier_semaphore()

    def greet(dev):
        pl.semaphore_signal(barrier, inc=1, device_id=dev, device_id_type=MESH)

    for d in range(1, EXPERTS):
        greet(expert_of(d))
    greet(right)
    greet(left)
    greet(partner)

    @pl.when(section + 1 < sections)
    def _():
        greet((section + 1, place))

    @pl.when(section > 0)
    def _():
        greet((section - 1, place))

    shape = (EXPERTS, CAP, 128)
    far = lax.broadcasted_iota(jnp.int32, shape, 0)
    which = lax.broadcasted_iota(jnp.int32, shape, 1)
    expert = (y + EXPERTS - far) & (EXPERTS - 1)

    def tables(ids, weights):
        seen = jnp.zeros(shape, jnp.int32)
        plain, weighted = [], []
        for t in range(TOK):
            has = jnp.zeros(shape, jnp.int32)
            weight = jnp.zeros(shape, jnp.float32)
            for k in range(ids.shape[2]):
                hit = expert == ids[0, t, k]
                has = jnp.where(hit, 1, has)
                weight = jnp.where(hit, weights[0, t, k], weight)
            here = jnp.where(seen == which, has, 0)
            plain.append(jnp.where(here == 1, 1.0, 0.0).astype(jnp.float32))
            weighted.append(jnp.where(here == 1, weight, 0.0))
            seen = seen + has
        return plain, weighted

    plain_f, weighted_f = tables(fexp, fwt)
    plain_b, weighted_b = tables(bexp, bwt)
    pack_table = (plain_f, weighted_b)
    join_table = (weighted_f, plain_b)

    copies = {}

    def pack(st, ch):
        values = tok[st, :, cols(ch)].astype(jnp.float32)
        for d in range(EXPERTS):
            total = None
            for t in range(TOK):
                term = pack_table[st][t][d][:, 0:1] * values[t : t + 1, :]
                total = term if total is None else total + term
            if d == 0:
                yrecv[st, ch, 0] = total.astype(jnp.bfloat16)
            else:
                ysend[st, ch, d] = total.astype(jnp.bfloat16)

    def send_slots(st, ch):
        for d in range(1, EXPERTS):
            copy = remote(
                ysend.at[st, ch, d],
                yrecv.at[st, ch, d],
                y_ss.at[st, ch, d],
                y_rs.at[st, ch, d],
                expert_of(d),
            )
            copy.start()
            copies["y", st, ch, d] = copy

    def spread(name, st, ch, number, src, dst, dev):
        copy = remote(src, dst, x_ss.at[st, ch, number], x_rs.at[st, ch, number], dev)
        copy.start()
        copies[name, st, ch] = copy

    def part(st, ch, gamma, delta):
        return rows.at[st, ch, pl.ds((gamma * RING + delta) * block, block), :]

    def halfpart(st, ch, gamma, delta, number):
        return rows.at[
            st, ch, pl.ds((gamma * RING + delta) * block, block), pl.ds(number * half, half)
        ]

    def stage_a(st, ch):
        for d in range(1, EXPERTS):
            copies["y", st, ch, d].wait_recv()
        own = yrecv[st, ch].astype(jnp.float32).reshape(block, wide)
        rows[st, ch, 0:block, :] = own.astype(jnp.bfloat16)
        spread("xr", st, ch, 0, part(st, ch, 0, 0), part(st, ch, 0, 3), right)
        spread("xl", st, ch, 1, part(st, ch, 0, 0), part(st, ch, 0, 1), left)
        spread("c0", st, ch, 2, part(st, ch, 0, 0), part(st, ch, 1, 0), partner)

    def stage_b(st, ch):
        copies["xl", st, ch].wait_recv()
        spread("hl", st, ch, 3, halfpart(st, ch, 0, 1, 0), halfpart(st, ch, 0, 2, 0), left)
        copies["xr", st, ch].wait_recv()
        spread("hr", st, ch, 4, halfpart(st, ch, 0, 3, 1), halfpart(st, ch, 0, 2, 1), right)
        spread("c1", st, ch, 5, part(st, ch, 0, 1), part(st, ch, 1, 1), partner)
        spread("c3", st, ch, 6, part(st, ch, 0, 3), part(st, ch, 1, 3), partner)

    def stage_c(st, ch):
        copies["hl", st, ch].wait_recv()
        copies["hr", st, ch].wait_recv()
        spread("c2", st, ch, 7, part(st, ch, 0, 2), part(st, ch, 1, 2), partner)

    def stage_d(st, ch):
        for name in ("c0", "c1", "c3", "c2"):
            copies[name, st, ch].wait_recv()
        arrived = rows[st, ch]
        if st == 0:
            if ch == 0:
                need("wg")
                need("wu")
            gate = jnp.dot(arrived, wg[cols(ch), :], preferred_element_type=jnp.float32)
            up = jnp.dot(arrived, wu[cols(ch), :], preferred_element_type=jnp.float32)
            if ch == 0:
                gacc[...] = gate
                uacc[...] = up
            else:
                gacc[...] += gate
                uacc[...] += up
        else:
            if ch == 0:
                need("wd")
            grad = lax.dot_general(arrived, wd[:, cols(ch)], LAST, preferred_element_type=jnp.float32)
            if ch == 0:
                hacc[...] = grad
            else:
                hacc[...] += grad

    def middle(st):
        if st == 0:
            gate = gacc[...]
            hid[...] = (gate * jax.nn.sigmoid(gate) * uacc[...]).astype(jnp.bfloat16)
        else:
            grad = hacc[...]
            need("sg")
            need("su")
            count = 2 * side
            mine = lax.broadcasted_iota(jnp.int32, (count, count), 0)
            theirs = lax.broadcasted_iota(jnp.int32, (count, count), 1)
            j = mine % CAP
            d = (mine // CAP) % EXPERTS
            delta = (mine // block) % RING
            gamma = mine // side
            ys = (y + d) % EXPERTS
            xs = (x + delta) % RING
            cs = (c + gamma) % CORES
            wanted = ((ys * RING + xs) * CORES + cs) * CAP + j
            order = jnp.where(wanted == theirs, 1.0, 0.0).astype(jnp.bfloat16)
            gate = jnp.dot(order, sg[...], preferred_element_type=jnp.float32)
            up = jnp.dot(order, su[...], preferred_element_type=jnp.float32)
            sig = jax.nn.sigmoid(gate)
            ggrad[...] = (grad * up * sig * (1.0 + gate * (1.0 - sig))).astype(jnp.bfloat16)
            ugrad[...] = (grad * (gate * sig)).astype(jnp.bfloat16)

    def back(name, st, ch, number, src, dst, dev):
        copy = remote(src, dst, r_ss.at[st, ch, number], r_rs.at[st, ch, number], dev)
        copy.start()
        copies[name, st, ch] = copy

    def stage_e(st, ch):
        if st == 0:
            if ch == 0:
                need("wd")
            partial = jnp.dot(hid[...], wd[:, cols(ch)], preferred_element_type=jnp.float32)
        else:
            partial = lax.dot_general(
                ggrad[...], wg[cols(ch), :], LAST, preferred_element_type=jnp.float32
            )
            partial = partial + lax.dot_general(
                ugrad[...], wu[cols(ch), :], LAST, preferred_element_type=jnp.float32
            )
        psend[st, ch] = partial[side:, :].astype(jnp.bfloat16)
        back("p", st, ch, 0, psend.at[st, ch], precv.at[st, ch], partner)
        pown[st, ch] = partial[:side, :]

    def stage_f(st, ch):
        copies["p", st, ch].wait_recv()
        far_rows = pl.ds(2 * block, block)
        t2s[st, ch] = (
            pown[st, ch, far_rows, :] + precv[st, ch, far_rows, :].astype(jnp.float32)
        ).astype(jnp.bfloat16)
        a, b = pl.ds(0, half), pl.ds(half, half)
        back("tl", st, ch, 1, t2s.at[st, ch, :, a], t2r.at[st, ch, :, a], left)
        back("tr", st, ch, 2, t2s.at[st, ch, :, b], t2r.at[st, ch, :, b], right)

    def chip_sum(st, ch, delta):
        some = pl.ds(delta * block, block)
        return pown[st, ch, some, :] + precv[st, ch, some, :].astype(jnp.float32)

    def stage_g(st, ch):
        to_left = chip_sum(st, ch, 3)
        copies["tl", st, ch].wait_recv()
        ts[st, ch, 0, :, 0:half] = (
            to_left[:, :half] + t2r[st, ch, :, 0:half].astype(jnp.float32)
        ).astype(jnp.bfloat16)
        ts[st, ch, 0, :, half:wide] = to_left[:, half:].astype(jnp.bfloat16)
        back("sl", st, ch, 3, ts.at[st, ch, 0], tr.at[st, ch, 0], left)
        to_right = chip_sum(st, ch, 1)
        copies["tr", st, ch].wait_recv()
        ts[st, ch, 1, :, 0:half] = to_right[:, :half].astype(jnp.bfloat16)
        ts[st, ch, 1, :, half:wide] = (
            to_right[:, half:] + t2r[st, ch, :, half:wide].astype(jnp.float32)
        ).astype(jnp.bfloat16)
        back("sr", st, ch, 4, ts.at[st, ch, 1], tr.at[st, ch, 1], right)

    def stage_h(st, ch):
        own = chip_sum(st, ch, 0)
        copies["sl", st, ch].wait_recv()
        copies["sr", st, ch].wait_recv()
        own = own + tr[st, ch, 0].astype(jnp.float32) + tr[st, ch, 1].astype(jnp.float32)
        for d in range(EXPERTS):
            piece = own[d * CAP : (d + 1) * CAP, :].astype(jnp.bfloat16)
            if d == 0:
                hr[st, ch, 0] = piece
            else:
                hs[st, ch, d] = piece
        for d in range(1, EXPERTS):
            copy = remote(
                hs.at[st, ch, d],
                hr.at[st, ch, d],
                h_ss.at[st, ch, d],
                h_rs.at[st, ch, d],
                source_of(d),
            )
            copy.start()
            copies["h", st, ch, d] = copy

    def handoff(st, ch):
        to = section + 1 if st == 0 else section - 1
        return remote(
            osend.at[st, ch],
            outs[st].at[0, :, cols(ch)],
            z_ss.at[st, ch],
            z_rs.at[st, ch],
            (to, place),
        )

    def gives(st):
        return section + 1 < sections if st == 0 else section > 0

    def takes(st):
        return section > 0 if st == 0 else section + 1 < sections

    def stage_i(st, ch):
        for d in range(1, EXPERTS):
            copies["h", st, ch, d].wait_recv()
        base = tok[st, :, cols(ch)].astype(jnp.float32)
        lines = []
        for t in range(TOK):
            total = None
            for d in range(EXPERTS):
                term = join_table[st][t][d][:, 0:1] * hr[st, ch, d].astype(jnp.float32)
                total = term if total is None else total + term
            lines.append(base[t : t + 1, :] + total[0:1, :] + total[1:2, :])
        osend[st, ch] = jnp.concatenate(lines, axis=0).astype(jnp.bfloat16)

        @pl.when(gives(st))
        def _():
            handoff(st, ch).start()

    chunks = [(st, ch) for st in range(2) for ch in range(cuts)]
    need("act")
    for ch in range(cuts):
        pack(0, ch)
    ends = (section + 1 < sections).astype(jnp.int32) + (section > 0).astype(jnp.int32)
    pl.semaphore_wait(barrier, EXPERTS - 1 + 3 + ends)

    for ch in range(cuts):
        send_slots(0, ch)
    need("cot")
    for ch in range(cuts):
        pack(1, ch)
        send_slots(1, ch)

    stages = (
        (stage_a, 0),
        (stage_b, 1),
        (stage_c, 2),
        (stage_d, 3),
        (stage_e, cuts + 3),
        (stage_f, cuts + 4),
        (stage_g, cuts + 5),
        (stage_h, cuts + 6),
        (stage_i, cuts + 8),
    )
    total_steps = len(chunks) + stages[-1][1]
    for step in range(total_steps):
        for stage, lag in stages:
            number = step - lag
            if 0 <= number < len(chunks):
                st, ch = chunks[number]
                stage(st, ch)
                if stage is stage_d and ch == cuts - 1:
                    middle(st)

    for st in range(2):

        @pl.when(takes(st))
        def _():
            for ch in range(cuts):
                handoff(st, ch).wait_recv()

        @pl.when(jnp.logical_not(takes(st)))
        def _():
            outs[st][...] = jnp.zeros_like(outs[st])

        @pl.when(gives(st))
        def _():
            for ch in range(cuts):
                handoff(st, ch).wait_send()

    for copy in copies.values():
        copy.wait_send()


def body(
    activations,
    cotangent,
    forward_experts,
    forward_weights,
    backward_experts,
    backward_weights,
    gate_weight,
    up_weight,
    down_weight,
    saved_gate,
    saved_up,
):
    cuts = CHUNKS
    tokens, width = activations.shape[1:]
    units = gate_weight.shape[1]
    slots = saved_gate.shape[1]
    wide = width // cuts
    block = EXPERTS * CAP
    side = RING * block
    anywhere = pl.BlockSpec(memory_space=pl.ANY)
    scalar = pl.BlockSpec(memory_space=pltpu.SMEM)
    vmem = pl.BlockSpec(memory_space=pltpu.VMEM)
    half = jnp.bfloat16
    full = jnp.float32
    dma = pltpu.SemaphoreType.DMA
    out = jax.ShapeDtypeStruct(activations.shape, half)
    return pl.pallas_call(
        functools.partial(kernel, cuts),
        out_shape=(out, out),
        in_specs=[anywhere, anywhere, scalar, scalar, scalar, scalar] + [anywhere] * 5,
        out_specs=(vmem, vmem),
        scratch_shapes=[
            pltpu.VMEM((2, tokens, width), half),
            pltpu.VMEM((width, units), half),
            pltpu.VMEM((width, units), half),
            pltpu.VMEM((units, width), half),
            pltpu.VMEM((slots, units), half),
            pltpu.VMEM((slots, units), half),
            pltpu.VMEM((2, cuts, EXPERTS, CAP, wide), half),
            pltpu.VMEM((2, cuts, EXPERTS, CAP, wide), half),
            pltpu.VMEM((2, cuts, slots, wide), half),
            pltpu.VMEM((slots, units), full),
            pltpu.VMEM((slots, units), full),
            pltpu.VMEM((slots, units), full),
            pltpu.VMEM((slots, units), half),
            pltpu.VMEM((slots, units), half),
            pltpu.VMEM((slots, units), half),
            pltpu.VMEM((2, cuts, side, wide), half),
            pltpu.VMEM((2, cuts, side, wide), half),
            pltpu.VMEM((2, cuts, side, wide), full),
            pltpu.VMEM((2, cuts, block, wide), half),
            pltpu.VMEM((2, cuts, block, wide), half),
            pltpu.VMEM((2, cuts, 2, block, wide), half),
            pltpu.VMEM((2, cuts, 2, block, wide), half),
            pltpu.VMEM((2, cuts, EXPERTS, CAP, wide), half),
            pltpu.VMEM((2, cuts, EXPERTS, CAP, wide), half),
            pltpu.VMEM((2, cuts, tokens, wide), half),
            dma((7,)),
            dma((2, cuts, EXPERTS)),
            dma((2, cuts, EXPERTS)),
            dma((2, cuts, 8)),
            dma((2, cuts, 8)),
            dma((2, cuts, 5)),
            dma((2, cuts, 5)),
            dma((2, cuts, EXPERTS)),
            dma((2, cuts, EXPERTS)),
            dma((2, cuts)),
            dma((2, cuts)),
        ],
        compiler_params=pltpu.CompilerParams(
            collective_id=0, has_side_effects=True, vmem_limit_bytes=60 * 1024 * 1024
        ),
    )(
        activations,
        cotangent,
        forward_experts,
        forward_weights,
        backward_experts,
        backward_weights,
        gate_weight,
        up_weight,
        down_weight,
        saved_gate,
        saved_up,
    )


def solution(mesh):
    in_specs = (
        P("pipe", "ep", None),
        P("pipe", "ep", None),
        P("pipe", "ep", None),
        P("pipe", "ep", None),
        P("pipe", "ep", None),
        P("pipe", "ep", None),
        P(None, "ep"),
        P(None, "ep"),
        P("ep", None),
        P("pipe", None, "ep"),
        P("pipe", None, "ep"),
    )
    out_specs = (P("pipe", "ep", None), P("pipe", "ep", None))
    return jax.shard_map(body, mesh=mesh, in_specs=in_specs, out_specs=out_specs, check_vma=False)
```

```python
import functools

import jax
import jax.numpy as jnp
from jax import lax
from jax.experimental import pallas as pl
from jax.experimental.pallas import tpu as pltpu
from jax.sharding import PartitionSpec as P

EXPERTS = 8
TOP = 4
CAP = 2
TOK = 3
CORES = 2
RING = 4
WIDTHS = ((1792, 1792, 1792, 1792), (1792, 1792, 1792, 1792))
ORDER = (
    "P00", "P01", "P02", "P03", "P10", "P11", "P12", "P13", "A00", "A01", "A02", "B00",
    "A03", "B01", "A10", "B02", "C00", "A11", "B03", "D00", "C01", "A12", "B10", "D01",
    "C02", "A13", "B11", "D02", "C03", "B12", "D03", "M00", "C10", "E00", "E01", "B13",
    "E02", "C11", "E03", "C12", "F00", "D10", "F01", "C13", "F02", "D11", "G00", "F03",
    "G01", "D12", "D13", "M10", "G02", "E10", "E11", "H00", "E12", "G03", "E13", "F10",
    "H01", "F11", "H02", "F12", "F13", "H03", "G10", "G11", "I00", "G12", "G13", "I01",
    "H10", "I02", "H11", "H12", "I03", "H13", "I10", "I11", "I12", "I13",
)
MESH = pl.DeviceIdType.MESH
LAST = (((1,), (1,)), ((), ()))


def kernel(
    widths,
    order,
    act_hbm,
    cot_hbm,
    fexp,
    fwt,
    bexp,
    bwt,
    wg_hbm,
    wu_hbm,
    wd_hbm,
    sg_hbm,
    su_hbm,
    out_f,
    out_b,
    tok,
    wg,
    wu,
    wd,
    sg,
    su,
    ysend,
    yrecv,
    rows,
    gacc,
    uacc,
    hacc,
    hid,
    ggrad,
    ugrad,
    psend,
    precv,
    pown,
    t2s,
    t2r,
    ts,
    tr,
    hs,
    hr,
    osend,
    in_sem,
    y_ss,
    y_rs,
    x_ss,
    x_rs,
    r_ss,
    r_rs,
    h_ss,
    h_rs,
    z_ss,
    z_rs,
):
    sections = lax.axis_size("pipe")
    section = lax.axis_index("pipe")
    place = lax.axis_index("ep")
    y = place // (RING * CORES)
    x = (place // CORES) % RING
    c = place % CORES
    block = EXPERTS * CAP
    side = RING * block
    outs = (out_f, out_b)

    def at(yy, xx, cc):
        return (section, (yy * RING + xx) * CORES + cc)

    right = at(y, (x + 1) % RING, c)
    left = at(y, (x + RING - 1) % RING, c)
    partner = at(y, x, 1 - c)

    def expert_of(d):
        return at((y + EXPERTS - d) % EXPERTS, x, c)

    def source_of(d):
        return at((y + d) % EXPERTS, x, c)

    def wide(st, ch):
        return widths[st][ch]

    def split(st, ch):
        return widths[st][ch] // 256 * 128

    def start_of(st, ch):
        return sum(widths[st][:ch])

    def cols(st, ch):
        return pl.ds(start_of(st, ch), wide(st, ch))

    def low(st, ch):
        return pl.ds(start_of(st, ch), split(st, ch))

    def high(st, ch):
        return pl.ds(start_of(st, ch) + split(st, ch), wide(st, ch) - split(st, ch))

    def remote(src, dst, ss, rs, dev):
        return pltpu.make_async_remote_copy(
            src_ref=src, dst_ref=dst, send_sem=ss, recv_sem=rs, device_id=dev, device_id_type=MESH
        )

    loads = {}

    def load(name, src, dst, number):
        copy = pltpu.make_async_copy(src, dst, in_sem.at[number])
        copy.start()
        loads[name] = copy

    def need(name):
        copy = loads.pop(name, None)
        if copy is not None:
            copy.wait()

    load("act", act_hbm.at[0], tok.at[0], 0)
    load("cot", cot_hbm.at[0], tok.at[1], 1)
    load("wg", wg_hbm, wg, 2)
    load("wu", wu_hbm, wu, 3)
    load("wd", wd_hbm, wd, 4)
    load("sg", sg_hbm.at[0], sg, 5)
    load("su", su_hbm.at[0], su, 6)

    barrier = pltpu.get_barrier_semaphore()

    def greet(dev):
        pl.semaphore_signal(barrier, inc=1, device_id=dev, device_id_type=MESH)

    for d in range(1, EXPERTS):
        greet(expert_of(d))
    greet(right)
    greet(left)
    greet(partner)

    @pl.when(section + 1 < sections)
    def _():
        greet((section + 1, place))

    @pl.when(section > 0)
    def _():
        greet((section - 1, place))

    shape = (EXPERTS, CAP, 128)
    far = lax.broadcasted_iota(jnp.int32, shape, 0)
    which = lax.broadcasted_iota(jnp.int32, shape, 1)
    expert = (y + EXPERTS - far) & (EXPERTS - 1)

    def tables(ids, weights):
        seen = jnp.zeros(shape, jnp.int32)
        plain, weighted = [], []
        for t in range(TOK):
            has = jnp.zeros(shape, jnp.int32)
            weight = jnp.zeros(shape, jnp.float32)
            for k in range(ids.shape[2]):
                hit = expert == ids[t, 0, k]
                has = jnp.where(hit, 1, has)
                weight = jnp.where(hit, weights[t, 0, k], weight)
            here = jnp.where(seen == which, has, 0)
            plain.append(jnp.where(here == 1, 1.0, 0.0).astype(jnp.float32))
            weighted.append(jnp.where(here == 1, weight, 0.0))
            seen = seen + has
        return plain, weighted

    plain_f, weighted_f = tables(fexp, fwt)
    plain_b, weighted_b = tables(bexp, bwt)
    pack_table = (plain_f, weighted_b)
    join_table = (weighted_f, plain_b)

    copies = {}

    def pack(st, ch):
        values = tok[st, :, cols(st, ch)].astype(jnp.float32)
        for d in range(EXPERTS):
            total = None
            for t in range(TOK):
                term = pack_table[st][t][d][:, 0:1] * values[t : t + 1, :]
                total = term if total is None else total + term
            if d == 0:
                yrecv[st, 0, :, cols(st, ch)] = total.astype(jnp.bfloat16)
            else:
                ysend[st, d, :, cols(st, ch)] = total.astype(jnp.bfloat16)

    def send_slots(st, ch):
        for d in range(1, EXPERTS):
            copy = remote(
                ysend.at[st, d, :, cols(st, ch)],
                yrecv.at[st, d, :, cols(st, ch)],
                y_ss.at[st, ch, d],
                y_rs.at[st, ch, d],
                expert_of(d),
            )
            copy.start()
            copies["y", st, ch, d] = copy

    def spread(name, st, ch, number, src, dst, dev):
        copy = remote(src, dst, x_ss.at[st, ch, number], x_rs.at[st, ch, number], dev)
        copy.start()
        copies[name, st, ch] = copy

    def part(st, ch, gamma, delta):
        return rows.at[st, pl.ds((gamma * RING + delta) * block, block), cols(st, ch)]

    def halfpart(st, ch, gamma, delta, number):
        some = low(st, ch) if number == 0 else high(st, ch)
        return rows.at[st, pl.ds((gamma * RING + delta) * block, block), some]

    def stage_a(st, ch):
        for d in range(1, EXPERTS):
            copies["y", st, ch, d].wait_recv()
        own = yrecv[st, :, :, cols(st, ch)].astype(jnp.float32).reshape(block, wide(st, ch))
        rows[st, 0:block, cols(st, ch)] = own.astype(jnp.bfloat16)
        spread("xr", st, ch, 0, part(st, ch, 0, 0), part(st, ch, 0, 3), right)
        spread("xl", st, ch, 1, part(st, ch, 0, 0), part(st, ch, 0, 1), left)
        spread("c0", st, ch, 2, part(st, ch, 0, 0), part(st, ch, 1, 0), partner)

    def stage_b(st, ch):
        copies["xl", st, ch].wait_recv()
        spread("hl", st, ch, 3, halfpart(st, ch, 0, 1, 0), halfpart(st, ch, 0, 2, 0), left)
        copies["xr", st, ch].wait_recv()
        spread("hr", st, ch, 4, halfpart(st, ch, 0, 3, 1), halfpart(st, ch, 0, 2, 1), right)
        spread("c1", st, ch, 5, part(st, ch, 0, 1), part(st, ch, 1, 1), partner)
        spread("c3", st, ch, 6, part(st, ch, 0, 3), part(st, ch, 1, 3), partner)

    def stage_c(st, ch):
        copies["hl", st, ch].wait_recv()
        copies["hr", st, ch].wait_recv()
        spread("c2", st, ch, 7, part(st, ch, 0, 2), part(st, ch, 1, 2), partner)

    def stage_d(st, ch):
        for name in ("c0", "c1", "c3", "c2"):
            copies[name, st, ch].wait_recv()
        arrived = rows[st, :, cols(st, ch)]
        if st == 0:
            if ch == 0:
                need("wg")
                need("wu")
            gate = jnp.dot(arrived, wg[cols(st, ch), :], preferred_element_type=jnp.float32)
            up = jnp.dot(arrived, wu[cols(st, ch), :], preferred_element_type=jnp.float32)
            if ch == 0:
                gacc[...] = gate
                uacc[...] = up
            else:
                gacc[...] += gate
                uacc[...] += up
        else:
            if ch == 0:
                need("wd")
            grad = lax.dot_general(arrived, wd[:, cols(st, ch)], LAST, preferred_element_type=jnp.float32)
            if ch == 0:
                hacc[...] = grad
            else:
                hacc[...] += grad

    def middle(st):
        if st == 0:
            gate = gacc[...]
            hid[...] = (gate * jax.nn.sigmoid(gate) * uacc[...]).astype(jnp.bfloat16)
        else:
            grad = hacc[...]
            need("sg")
            need("su")
            count = 2 * side
            mine = lax.broadcasted_iota(jnp.int32, (count, count), 0)
            theirs = lax.broadcasted_iota(jnp.int32, (count, count), 1)
            j = mine % CAP
            d = (mine // CAP) % EXPERTS
            delta = (mine // block) % RING
            gamma = mine // side
            ys = (y + d) % EXPERTS
            xs = (x + delta) % RING
            cs = (c + gamma) % CORES
            wanted = ((ys * RING + xs) * CORES + cs) * CAP + j
            order = jnp.where(wanted == theirs, 1.0, 0.0).astype(jnp.bfloat16)
            gate = jnp.dot(order, sg[...], preferred_element_type=jnp.float32)
            up = jnp.dot(order, su[...], preferred_element_type=jnp.float32)
            sig = jax.nn.sigmoid(gate)
            ggrad[...] = (grad * up * sig * (1.0 + gate * (1.0 - sig))).astype(jnp.bfloat16)
            ugrad[...] = (grad * (gate * sig)).astype(jnp.bfloat16)

    def back(name, st, ch, number, src, dst, dev):
        copy = remote(src, dst, r_ss.at[st, ch, number], r_rs.at[st, ch, number], dev)
        copy.start()
        copies[name, st, ch] = copy

    def stage_e(st, ch):
        if st == 0:
            if ch == 0:
                need("wd")
            partial = jnp.dot(hid[...], wd[:, cols(st, ch)], preferred_element_type=jnp.float32)
        else:
            partial = lax.dot_general(
                ggrad[...], wg[cols(st, ch), :], LAST, preferred_element_type=jnp.float32
            )
            partial = partial + lax.dot_general(
                ugrad[...], wu[cols(st, ch), :], LAST, preferred_element_type=jnp.float32
            )
        psend[st, :, cols(st, ch)] = partial[side:, :].astype(jnp.bfloat16)
        here = cols(st, ch)
        back("p", st, ch, 0, psend.at[st, :, here], precv.at[st, :, here], partner)
        pown[st, :, cols(st, ch)] = partial[:side, :]

    def chip_sum(st, delta, some):
        lines = pl.ds(delta * block, block)
        return pown[st, lines, some] + precv[st, lines, some].astype(jnp.float32)

    def stage_f(st, ch):
        copies["p", st, ch].wait_recv()
        t2s[st, :, cols(st, ch)] = chip_sum(st, 2, cols(st, ch)).astype(jnp.bfloat16)
        a, b = low(st, ch), high(st, ch)
        back("tl", st, ch, 1, t2s.at[st, :, a], t2r.at[st, :, a], left)
        back("tr", st, ch, 2, t2s.at[st, :, b], t2r.at[st, :, b], right)

    def stage_g(st, ch):
        here, a, b = cols(st, ch), low(st, ch), high(st, ch)
        ts[st, 0, :, b] = chip_sum(st, 3, b).astype(jnp.bfloat16)
        copies["tl", st, ch].wait_recv()
        ts[st, 0, :, a] = (chip_sum(st, 3, a) + t2r[st, :, a].astype(jnp.float32)).astype(
            jnp.bfloat16
        )
        back("sl", st, ch, 3, ts.at[st, 0, :, here], tr.at[st, 0, :, here], left)
        ts[st, 1, :, a] = chip_sum(st, 1, a).astype(jnp.bfloat16)
        copies["tr", st, ch].wait_recv()
        ts[st, 1, :, b] = (chip_sum(st, 1, b) + t2r[st, :, b].astype(jnp.float32)).astype(
            jnp.bfloat16
        )
        back("sr", st, ch, 4, ts.at[st, 1, :, here], tr.at[st, 1, :, here], right)

    def stage_h(st, ch):
        here = cols(st, ch)
        copies["sl", st, ch].wait_recv()
        copies["sr", st, ch].wait_recv()
        own = chip_sum(st, 0, here) + tr[st, 0, :, here].astype(jnp.float32)
        own = own + tr[st, 1, :, here].astype(jnp.float32)
        for d in range(EXPERTS):
            piece = own[d * CAP : (d + 1) * CAP, :].astype(jnp.bfloat16)
            if d == 0:
                hr[st, 0, :, here] = piece
            else:
                hs[st, d, :, here] = piece
        for d in range(1, EXPERTS):
            copy = remote(
                hs.at[st, d, :, here],
                hr.at[st, d, :, here],
                h_ss.at[st, ch, d],
                h_rs.at[st, ch, d],
                source_of(d),
            )
            copy.start()
            copies["h", st, ch, d] = copy

    def handoff(st, ch):
        to = section + 1 if st == 0 else section - 1
        return remote(
            osend.at[st, :, cols(st, ch)],
            outs[st].at[0, :, cols(st, ch)],
            z_ss.at[st, ch],
            z_rs.at[st, ch],
            (to, place),
        )

    def gives(st):
        return section + 1 < sections if st == 0 else section > 0

    def takes(st):
        return section > 0 if st == 0 else section + 1 < sections

    def stage_i(st, ch):
        for d in range(1, EXPERTS):
            copies["h", st, ch, d].wait_recv()
        base = tok[st, :, cols(st, ch)].astype(jnp.float32)
        lines = []
        for t in range(TOK):
            total = None
            for d in range(EXPERTS):
                term = join_table[st][t][d][:, 0:1] * hr[st, d, :, cols(st, ch)].astype(jnp.float32)
                total = term if total is None else total + term
            lines.append(base[t : t + 1, :] + total[0:1, :] + total[1:2, :])
        osend[st, :, cols(st, ch)] = jnp.concatenate(lines, axis=0).astype(jnp.bfloat16)

        @pl.when(gives(st))
        def _():
            handoff(st, ch).start()

    ends = (section + 1 < sections).astype(jnp.int32) + (section > 0).astype(jnp.int32)
    stages = {
        "A": stage_a,
        "B": stage_b,
        "C": stage_c,
        "D": stage_d,
        "E": stage_e,
        "F": stage_f,
        "G": stage_g,
        "H": stage_h,
        "I": stage_i,
    }
    greeted = False
    for step in order:
        kind, st, ch = step[0], int(step[1]), int(step[2])
        if kind == "P":
            need("act" if st == 0 else "cot")
            pack(st, ch)
            if not greeted:
                pl.semaphore_wait(barrier, EXPERTS - 1 + 3 + ends)
                greeted = True
            send_slots(st, ch)
        elif kind == "M":
            middle(st)
        else:
            stages[kind](st, ch)

    for st in range(2):

        @pl.when(takes(st))
        def _():
            for ch in range(len(widths[st])):
                handoff(st, ch).wait_recv()

        @pl.when(jnp.logical_not(takes(st)))
        def _():
            outs[st][...] = jnp.zeros_like(outs[st])

        @pl.when(gives(st))
        def _():
            for ch in range(len(widths[st])):
                handoff(st, ch).wait_send()

    for copy in copies.values():
        copy.wait_send()


def body(
    activations,
    cotangent,
    forward_experts,
    forward_weights,
    backward_experts,
    backward_weights,
    gate_weight,
    up_weight,
    down_weight,
    saved_gate,
    saved_up,
):
    cuts = max(len(WIDTHS[0]), len(WIDTHS[1]))
    tokens, width = activations.shape[1:]
    units = gate_weight.shape[1]
    slots = saved_gate.shape[1]
    block = EXPERTS * CAP
    side = RING * block
    anywhere = pl.BlockSpec(memory_space=pl.ANY)
    scalar = pl.BlockSpec(memory_space=pltpu.SMEM)
    vmem = pl.BlockSpec(memory_space=pltpu.VMEM)
    half = jnp.bfloat16
    full = jnp.float32
    dma = pltpu.SemaphoreType.DMA
    out = jax.ShapeDtypeStruct(activations.shape, half)
    return pl.pallas_call(
        functools.partial(kernel, WIDTHS, ORDER),
        out_shape=(out, out),
        in_specs=[anywhere, anywhere, scalar, scalar, scalar, scalar] + [anywhere] * 5,
        out_specs=(vmem, vmem),
        scratch_shapes=[
            pltpu.VMEM((2, tokens, width), half),
            pltpu.VMEM((width, units), half),
            pltpu.VMEM((width, units), half),
            pltpu.VMEM((units, width), half),
            pltpu.VMEM((slots, units), half),
            pltpu.VMEM((slots, units), half),
            pltpu.VMEM((2, EXPERTS, CAP, width), half),
            pltpu.VMEM((2, EXPERTS, CAP, width), half),
            pltpu.VMEM((2, slots, width), half),
            pltpu.VMEM((slots, units), full),
            pltpu.VMEM((slots, units), full),
            pltpu.VMEM((slots, units), full),
            pltpu.VMEM((slots, units), half),
            pltpu.VMEM((slots, units), half),
            pltpu.VMEM((slots, units), half),
            pltpu.VMEM((2, side, width), half),
            pltpu.VMEM((2, side, width), half),
            pltpu.VMEM((2, side, width), full),
            pltpu.VMEM((2, block, width), half),
            pltpu.VMEM((2, block, width), half),
            pltpu.VMEM((2, 2, block, width), half),
            pltpu.VMEM((2, 2, block, width), half),
            pltpu.VMEM((2, EXPERTS, CAP, width), half),
            pltpu.VMEM((2, EXPERTS, CAP, width), half),
            pltpu.VMEM((2, tokens, width), half),
            dma((7,)),
            dma((2, cuts, EXPERTS)),
            dma((2, cuts, EXPERTS)),
            dma((2, cuts, 8)),
            dma((2, cuts, 8)),
            dma((2, cuts, 5)),
            dma((2, cuts, 5)),
            dma((2, cuts, EXPERTS)),
            dma((2, cuts, EXPERTS)),
            dma((2, cuts)),
            dma((2, cuts)),
        ],
        compiler_params=pltpu.CompilerParams(
            collective_id=0, has_side_effects=True, vmem_limit_bytes=60 * 1024 * 1024
        ),
    )(
        activations,
        cotangent,
        forward_experts.transpose(1, 0, 2),
        forward_weights.transpose(1, 0, 2),
        backward_experts.transpose(1, 0, 2),
        backward_weights.transpose(1, 0, 2),
        gate_weight,
        up_weight,
        down_weight,
        saved_gate,
        saved_up,
    )


def solution(mesh):
    in_specs = (
        P("pipe", "ep", None),
        P("pipe", "ep", None),
        P("pipe", "ep", None),
        P("pipe", "ep", None),
        P("pipe", "ep", None),
        P("pipe", "ep", None),
        P(None, "ep"),
        P(None, "ep"),
        P("ep", None),
        P("pipe", None, "ep"),
        P("pipe", None, "ep"),
    )
    out_specs = (P("pipe", "ep", None), P("pipe", "ep", None))
    return jax.shard_map(body, mesh=mesh, in_specs=in_specs, out_specs=out_specs, check_vma=False)
```

```python
import functools

import jax
import jax.numpy as jnp
from jax import lax
from jax.experimental import pallas as pl
from jax.experimental.pallas import tpu as pltpu
from jax.sharding import PartitionSpec as P

EXPERTS = 8
TOP = 4
CAP = 2
TOK = 3
CORES = 2
RING = 4
WIDTHS = ((2304, 2560, 2304), (2304, 2560, 2304))
FAR = ((0,) * 8, (0,) * 8)
FARB = ((0,) * 8, (0,) * 8)
ORDER = (
    "P00", "P01", "P02", "P10", "A00", "P11", "A01", "P12", "A02", "B00", "A10", "B01",
    "B02", "C00", "A11", "A12", "C01", "C02", "D00", "B10", "D01", "D02", "B11", "M00",
    "E00", "B12", "C10", "E01", "F00", "C11", "D10", "C12", "E02", "F01", "D11", "G00",
    "D12", "M10", "F02", "E10", "G01", "E11", "E12", "F10", "G02", "F11", "H00", "F12",
    "G10", "H01", "H02", "G11", "G12", "H10", "H11", "H12", "I02", "I00", "I10", "I01",
    "I11", "I12",
)
MESH = pl.DeviceIdType.MESH
LAST = (((1,), (1,)), ((), ()))


def kernel(
    widths,
    order,
    act_hbm,
    cot_hbm,
    fexp,
    fwt,
    bexp,
    bwt,
    wg_hbm,
    wu_hbm,
    wd_hbm,
    sg_hbm,
    su_hbm,
    out_f,
    out_b,
    tok,
    wg,
    wu,
    wd,
    sg,
    su,
    ysend,
    yrecv,
    rows,
    gacc,
    uacc,
    hacc,
    hid,
    ggrad,
    ugrad,
    psend,
    precv,
    pown,
    t2s,
    t2r,
    ts,
    tr,
    hs,
    hr,
    base,
    tsend,
    trecv,
    in_sem,
    y_ss,
    y_rs,
    x_ss,
    x_rs,
    r_ss,
    r_rs,
    h_ss,
    h_rs,
    b_ss,
    b_rs,
):
    sections = lax.axis_size("pipe")
    section = lax.axis_index("pipe")
    place = lax.axis_index("ep")
    y = place // (RING * CORES)
    x = (place // CORES) % RING
    c = place % CORES
    block = EXPERTS * CAP
    side = RING * block
    outs = (out_f, out_b)

    def at(yy, xx, cc):
        return (section, (yy * RING + xx) * CORES + cc)

    right = at(y, (x + 1) % RING, c)
    left = at(y, (x + RING - 1) % RING, c)
    partner = at(y, x, 1 - c)
    opposite = at(y, (x + 2) % RING, c)

    def expert_of(d):
        return at((y + EXPERTS - d) % EXPERTS, x, c)

    def ahead(st):
        return section + 1 if st == 0 else section - 1

    def behind(st):
        return section - 1 if st == 0 else section + 1

    def gives(st):
        return section + 1 < sections if st == 0 else section > 0

    def takes(st):
        return section > 0 if st == 0 else section + 1 < sections

    def heir_of(st, d):
        return (ahead(st), (((y + d) % EXPERTS) * RING + x) * CORES + c)

    def giver_of(st, d):
        return (behind(st), (((y + EXPERTS - d) % EXPERTS) * RING + x) * CORES + c)

    def wide(st, ch):
        return widths[st][ch]

    def split(st, ch):
        return widths[st][ch] // 256 * 128

    def start_of(st, ch):
        return sum(widths[st][:ch])

    def cols(st, ch):
        return pl.ds(start_of(st, ch), wide(st, ch))

    def low(st, ch):
        return pl.ds(start_of(st, ch), split(st, ch))

    def high(st, ch):
        return pl.ds(start_of(st, ch) + split(st, ch), wide(st, ch) - split(st, ch))

    def remote(src, dst, ss, rs, dev):
        return pltpu.make_async_remote_copy(
            src_ref=src, dst_ref=dst, send_sem=ss, recv_sem=rs, device_id=dev, device_id_type=MESH
        )

    loads = {}

    def load(name, src, dst, number):
        copy = pltpu.make_async_copy(src, dst, in_sem.at[number])
        copy.start()
        loads[name] = copy

    def need(name):
        copy = loads.pop(name, None)
        if copy is not None:
            copy.wait()

    load("act", act_hbm.at[0], tok.at[0], 0)
    load("cot", cot_hbm.at[0], tok.at[1], 1)
    load("wg", wg_hbm, wg, 2)
    load("wu", wu_hbm, wu, 3)
    load("wd", wd_hbm, wd, 4)
    load("sg", sg_hbm.at[0], sg, 5)
    load("su", su_hbm.at[0], su, 6)

    barrier = pltpu.get_barrier_semaphore()

    def greet(dev):
        pl.semaphore_signal(barrier, inc=1, device_id=dev, device_id_type=MESH)

    for d in range(1, EXPERTS):
        greet(expert_of(d))
    greet(right)
    greet(left)
    greet(partner)

    greet(opposite)
    for st in range(2):

        @pl.when(gives(st))
        def _():
            for d in range(EXPERTS):
                greet(heir_of(st, d))

    for st in range(2):

        @pl.when(takes(st))
        def _():
            for d in range(EXPERTS):
                greet(giver_of(st, d))

    shape = (EXPERTS, CAP, 128)
    far = lax.broadcasted_iota(jnp.int32, shape, 0)
    which = lax.broadcasted_iota(jnp.int32, shape, 1)
    expert = (y + EXPERTS - far) & (EXPERTS - 1)

    def tables(ids, weights):
        seen = jnp.zeros(shape, jnp.int32)
        plain, weighted = [], []
        for t in range(TOK):
            has = jnp.zeros(shape, jnp.int32)
            weight = jnp.zeros(shape, jnp.float32)
            for k in range(ids.shape[2]):
                hit = expert == ids[t, 0, k]
                has = jnp.where(hit, 1, has)
                weight = jnp.where(hit, weights[t, 0, k], weight)
            here = jnp.where(seen == which, has, 0)
            plain.append(jnp.where(here == 1, 1.0, 0.0).astype(jnp.float32))
            weighted.append(jnp.where(here == 1, weight, 0.0))
            seen = seen + has
        return plain, weighted

    plain_f, weighted_f = tables(fexp, fwt)
    plain_b, weighted_b = tables(bexp, bwt)
    pack_table = (plain_f, weighted_b)
    for t in range(TOK):
        tsend[0, t] = weighted_f[t]
        tsend[1, t] = plain_b[t]

    copies = {}

    def pack(st, ch):
        values = tok[st, :, cols(st, ch)].astype(jnp.float32)
        for d in range(EXPERTS):
            total = None
            for t in range(TOK):
                term = pack_table[st][t][d][:, 0:1] * values[t : t + 1, :]
                total = term if total is None else total + term
            if d == 0:
                yrecv[st, 0, :, cols(st, ch)] = total.astype(jnp.bfloat16)
            else:
                ysend[st, d, :, cols(st, ch)] = total.astype(jnp.bfloat16)

    def send_slots(st, ch):
        for d in range(1, EXPERTS):
            copy = remote(
                ysend.at[st, d, :, cols(st, ch)],
                yrecv.at[st, d, :, cols(st, ch)],
                y_ss.at[st, ch, d],
                y_rs.at[st, ch, d],
                expert_of(d),
            )
            copy.start()
            copies["y", st, ch, d] = copy

    def spread(name, st, ch, number, src, dst, dev):
        copy = remote(src, dst, x_ss.at[st, ch, number], x_rs.at[st, ch, number], dev)
        copy.start()
        copies[name, st, ch] = copy

    def part(st, ch, gamma, delta):
        return rows.at[st, pl.ds((gamma * RING + delta) * block, block), cols(st, ch)]

    def halfpart(st, ch, gamma, delta, number):
        some = low(st, ch) if number == 0 else high(st, ch)
        return rows.at[st, pl.ds((gamma * RING + delta) * block, block), some]

    def stage_a(st, ch):
        for d in range(1, EXPERTS):
            copies["y", st, ch, d].wait_recv()
        own = yrecv[st, :, :, cols(st, ch)].astype(jnp.float32).reshape(block, wide(st, ch))
        rows[st, 0:block, cols(st, ch)] = own.astype(jnp.bfloat16)
        spread("xr", st, ch, 0, part(st, ch, 0, 0), part(st, ch, 0, 3), right)
        spread("xl", st, ch, 1, part(st, ch, 0, 0), part(st, ch, 0, 1), left)
        if FAR[st][ch]:
            spread("xo", st, ch, 3, part(st, ch, 0, 0), part(st, ch, 0, 2), opposite)
        spread("c0", st, ch, 2, part(st, ch, 0, 0), part(st, ch, 1, 0), partner)

    def stage_b(st, ch):
        copies["xl", st, ch].wait_recv()
        if not FAR[st][ch]:
            spread("hl", st, ch, 3, halfpart(st, ch, 0, 1, 0), halfpart(st, ch, 0, 2, 0), left)
        copies["xr", st, ch].wait_recv()
        if not FAR[st][ch]:
            spread("hr", st, ch, 4, halfpart(st, ch, 0, 3, 1), halfpart(st, ch, 0, 2, 1), right)
        spread("c1", st, ch, 5, part(st, ch, 0, 1), part(st, ch, 1, 1), partner)
        spread("c3", st, ch, 6, part(st, ch, 0, 3), part(st, ch, 1, 3), partner)

    def stage_c(st, ch):
        for name in ("xo",) if FAR[st][ch] else ("hl", "hr"):
            copies[name, st, ch].wait_recv()
        spread("c2", st, ch, 7, part(st, ch, 0, 2), part(st, ch, 1, 2), partner)

    def stage_d(st, ch):
        for name in ("c0", "c1", "c3", "c2"):
            copies[name, st, ch].wait_recv()
        arrived = rows[st, :, cols(st, ch)]
        if st == 0:
            if ch == 0:
                need("wg")
                need("wu")
            gate = jnp.dot(arrived, wg[cols(st, ch), :], preferred_element_type=jnp.float32)
            up = jnp.dot(arrived, wu[cols(st, ch), :], preferred_element_type=jnp.float32)
            if ch == 0:
                gacc[...] = gate
                uacc[...] = up
            else:
                gacc[...] += gate
                uacc[...] += up
        else:
            if ch == 0:
                need("wd")
            grad = lax.dot_general(arrived, wd[:, cols(st, ch)], LAST, preferred_element_type=jnp.float32)
            if ch == 0:
                hacc[...] = grad
            else:
                hacc[...] += grad

    def middle(st):
        if st == 0:
            gate = gacc[...]
            hid[...] = (gate * jax.nn.sigmoid(gate) * uacc[...]).astype(jnp.bfloat16)
        else:
            grad = hacc[...]
            need("sg")
            need("su")
            count = 2 * side
            mine = lax.broadcasted_iota(jnp.int32, (count, count), 0)
            theirs = lax.broadcasted_iota(jnp.int32, (count, count), 1)
            j = mine % CAP
            d = (mine // CAP) % EXPERTS
            delta = (mine // block) % RING
            gamma = mine // side
            ys = (y + d) % EXPERTS
            xs = (x + delta) % RING
            cs = (c + gamma) % CORES
            wanted = ((ys * RING + xs) * CORES + cs) * CAP + j
            order = jnp.where(wanted == theirs, 1.0, 0.0).astype(jnp.bfloat16)
            gate = jnp.dot(order, sg[...], preferred_element_type=jnp.float32)
            up = jnp.dot(order, su[...], preferred_element_type=jnp.float32)
            sig = jax.nn.sigmoid(gate)
            ggrad[...] = (grad * up * sig * (1.0 + gate * (1.0 - sig))).astype(jnp.bfloat16)
            ugrad[...] = (grad * (gate * sig)).astype(jnp.bfloat16)

    def back(name, st, ch, number, src, dst, dev):
        copy = remote(src, dst, r_ss.at[st, ch, number], r_rs.at[st, ch, number], dev)
        copy.start()
        copies[name, st, ch] = copy

    def stage_e(st, ch):
        if st == 0:
            if ch == 0:
                need("wd")
            partial = jnp.dot(hid[...], wd[:, cols(st, ch)], preferred_element_type=jnp.float32)
        else:
            partial = lax.dot_general(
                ggrad[...], wg[cols(st, ch), :], LAST, preferred_element_type=jnp.float32
            )
            partial = partial + lax.dot_general(
                ugrad[...], wu[cols(st, ch), :], LAST, preferred_element_type=jnp.float32
            )
        psend[st, :, cols(st, ch)] = partial[side:, :].astype(jnp.bfloat16)
        here = cols(st, ch)
        back("p", st, ch, 0, psend.at[st, :, here], precv.at[st, :, here], partner)
        pown[st, :, cols(st, ch)] = partial[:side, :]

    def chip_sum(st, delta, some):
        lines = pl.ds(delta * block, block)
        return pown[st, lines, some] + precv[st, lines, some].astype(jnp.float32)

    def stage_f(st, ch):
        copies["p", st, ch].wait_recv()
        here = cols(st, ch)
        t2s[st, :, here] = chip_sum(st, 2, here).astype(jnp.bfloat16)
        if FARB[st][ch]:
            back("to", st, ch, 1, t2s.at[st, :, here], t2r.at[st, :, here], opposite)
            ts[st, 0, :, here] = chip_sum(st, 3, here).astype(jnp.bfloat16)
            back("sl", st, ch, 3, ts.at[st, 0, :, here], tr.at[st, 0, :, here], left)
            ts[st, 1, :, here] = chip_sum(st, 1, here).astype(jnp.bfloat16)
            back("sr", st, ch, 4, ts.at[st, 1, :, here], tr.at[st, 1, :, here], right)
        else:
            a, b = low(st, ch), high(st, ch)
            back("tl", st, ch, 1, t2s.at[st, :, a], t2r.at[st, :, a], left)
            back("tr", st, ch, 2, t2s.at[st, :, b], t2r.at[st, :, b], right)

    def stage_g(st, ch):
        if FARB[st][ch]:
            return
        here, a, b = cols(st, ch), low(st, ch), high(st, ch)
        ts[st, 0, :, b] = chip_sum(st, 3, b).astype(jnp.bfloat16)
        copies["tl", st, ch].wait_recv()
        ts[st, 0, :, a] = (chip_sum(st, 3, a) + t2r[st, :, a].astype(jnp.float32)).astype(
            jnp.bfloat16
        )
        back("sl", st, ch, 3, ts.at[st, 0, :, here], tr.at[st, 0, :, here], left)
        ts[st, 1, :, a] = chip_sum(st, 1, a).astype(jnp.bfloat16)
        copies["tr", st, ch].wait_recv()
        ts[st, 1, :, b] = (chip_sum(st, 1, b) + t2r[st, :, b].astype(jnp.float32)).astype(
            jnp.bfloat16
        )
        back("sr", st, ch, 4, ts.at[st, 1, :, here], tr.at[st, 1, :, here], right)

    def stage_h(st, ch):
        here = cols(st, ch)
        copies["sl", st, ch].wait_recv()
        copies["sr", st, ch].wait_recv()
        own = chip_sum(st, 0, here) + tr[st, 0, :, here].astype(jnp.float32)
        own = own + tr[st, 1, :, here].astype(jnp.float32)
        if FARB[st][ch]:
            copies["to", st, ch].wait_recv()
            own = own + t2r[st, :, here].astype(jnp.float32)
        for d in range(EXPERTS):
            hs[st, d, :, here] = own[d * CAP : (d + 1) * CAP, :].astype(jnp.bfloat16)

        @pl.when(gives(st))
        def _():
            for d in range(EXPERTS):
                homeward(st, ch, d).start()

    def homeward(st, ch, d):
        here = cols(st, ch)
        return remote(
            hs.at[st, d, :, here],
            hr.at[st, d, :, here],
            h_ss.at[st, ch, d],
            h_rs.at[st, ch, d],
            heir_of(st, d),
        )

    def footing(st):
        to = (ahead(st), place)
        return (
            remote(tok.at[st], base.at[st], b_ss.at[st, 0], b_rs.at[st, 0], to),
            remote(tsend.at[st], trecv.at[st], b_ss.at[st, 1], b_rs.at[st, 1], to),
        )

    def stage_i(st, ch):
        here = cols(st, ch)

        @pl.when(takes(st))
        def _():
            if ("base", st) not in seen_base:
                seen_base.add(("base", st))
                for copy in footing(st):
                    copy.wait_recv()
            for d in range(EXPERTS):
                homeward(st, ch, d).wait_recv()
            ground = base[st, :, here].astype(jnp.float32)
            lines = []
            for t in range(TOK):
                total = None
                for d in range(EXPERTS):
                    term = trecv[st, t, d][:, 0:1] * hr[st, d, :, here].astype(jnp.float32)
                    total = term if total is None else total + term
                lines.append(ground[t : t + 1, :] + total[0:1, :] + total[1:2, :])
            outs[st][0, :, here] = jnp.concatenate(lines, axis=0).astype(jnp.bfloat16)

    seen_base = set()

    ends = (section + 1 < sections).astype(jnp.int32) + (section > 0).astype(jnp.int32)
    stages = {
        "A": stage_a,
        "B": stage_b,
        "C": stage_c,
        "D": stage_d,
        "E": stage_e,
        "F": stage_f,
        "G": stage_g,
        "H": stage_h,
        "I": stage_i,
    }
    greeted = False
    for step in order:
        kind, st, ch = step[0], int(step[1]), int(step[2])
        if kind == "P":
            need("act" if st == 0 else "cot")
            pack(st, ch)
            if not greeted:
                pl.semaphore_wait(barrier, EXPERTS - 1 + 4 + 2 * EXPERTS * ends)
                greeted = True
            send_slots(st, ch)
            if ch == len(widths[st]) - 1:

                @pl.when(gives(st))
                def _():
                    for copy in footing(st):
                        copy.start()

        elif kind == "M":
            middle(st)
        else:
            stages[kind](st, ch)

    for st in range(2):

        @pl.when(jnp.logical_not(takes(st)))
        def _():
            outs[st][...] = jnp.zeros_like(outs[st])

        @pl.when(gives(st))
        def _():
            for copy in footing(st):
                copy.wait_send()
            for ch in range(len(widths[st])):
                for d in range(EXPERTS):
                    homeward(st, ch, d).wait_send()

    for copy in copies.values():
        copy.wait_send()


def settle(first, second, first_out, second_out):
    first_out[...] = first[...]
    second_out[...] = second[...]


def body(
    activations,
    cotangent,
    forward_experts,
    forward_weights,
    backward_experts,
    backward_weights,
    gate_weight,
    up_weight,
    down_weight,
    saved_gate,
    saved_up,
):
    cuts = max(len(WIDTHS[0]), len(WIDTHS[1]))
    tokens, width = activations.shape[1:]
    units = gate_weight.shape[1]
    slots = saved_gate.shape[1]
    block = EXPERTS * CAP
    side = RING * block
    anywhere = pl.BlockSpec(memory_space=pl.ANY)
    scalar = pl.BlockSpec(memory_space=pltpu.SMEM)
    vmem = pl.BlockSpec(memory_space=pltpu.VMEM)
    half = jnp.bfloat16
    full = jnp.float32
    dma = pltpu.SemaphoreType.DMA
    out = jax.ShapeDtypeStruct(activations.shape, half)
    results = pl.pallas_call(
        functools.partial(kernel, WIDTHS, ORDER),
        out_shape=(out, out),
        in_specs=[anywhere, anywhere, scalar, scalar, scalar, scalar] + [anywhere] * 5,
        out_specs=(vmem, vmem),
        scratch_shapes=[
            pltpu.VMEM((2, tokens, width), half),
            pltpu.VMEM((width, units), half),
            pltpu.VMEM((width, units), half),
            pltpu.VMEM((units, width), half),
            pltpu.VMEM((slots, units), half),
            pltpu.VMEM((slots, units), half),
            pltpu.VMEM((2, EXPERTS, CAP, width), half),
            pltpu.VMEM((2, EXPERTS, CAP, width), half),
            pltpu.VMEM((2, slots, width), half),
            pltpu.VMEM((slots, units), full),
            pltpu.VMEM((slots, units), full),
            pltpu.VMEM((slots, units), full),
            pltpu.VMEM((slots, units), half),
            pltpu.VMEM((slots, units), half),
            pltpu.VMEM((slots, units), half),
            pltpu.VMEM((2, side, width), half),
            pltpu.VMEM((2, side, width), half),
            pltpu.VMEM((2, side, width), full),
            pltpu.VMEM((2, block, width), half),
            pltpu.VMEM((2, block, width), half),
            pltpu.VMEM((2, 2, block, width), half),
            pltpu.VMEM((2, 2, block, width), half),
            pltpu.VMEM((2, EXPERTS, CAP, width), half),
            pltpu.VMEM((2, EXPERTS, CAP, width), half),
            pltpu.VMEM((2, tokens, width), half),
            pltpu.VMEM((2, tokens, EXPERTS, CAP, 128), full),
            pltpu.VMEM((2, tokens, EXPERTS, CAP, 128), full),
            dma((7,)),
            dma((2, cuts, EXPERTS)),
            dma((2, cuts, EXPERTS)),
            dma((2, cuts, 8)),
            dma((2, cuts, 8)),
            dma((2, cuts, 5)),
            dma((2, cuts, 5)),
            dma((2, cuts, EXPERTS)),
            dma((2, cuts, EXPERTS)),
            dma((2, 2)),
            dma((2, 2)),
        ],
        compiler_params=pltpu.CompilerParams(
            collective_id=0, has_side_effects=True, vmem_limit_bytes=60 * 1024 * 1024
        ),
    )(
        activations,
        cotangent,
        forward_experts.transpose(1, 0, 2),
        forward_weights.transpose(1, 0, 2),
        backward_experts.transpose(1, 0, 2),
        backward_weights.transpose(1, 0, 2),
        gate_weight,
        up_weight,
        down_weight,
        saved_gate,
        saved_up,
    )
    return pl.pallas_call(
        settle,
        out_shape=(out, out),
        in_specs=[vmem, vmem],
        out_specs=(vmem, vmem),
    )(*results)


def solution(mesh):
    in_specs = (
        P("pipe", "ep", None),
        P("pipe", "ep", None),
        P("pipe", "ep", None),
        P("pipe", "ep", None),
        P("pipe", "ep", None),
        P("pipe", "ep", None),
        P(None, "ep"),
        P(None, "ep"),
        P("ep", None),
        P("pipe", None, "ep"),
        P("pipe", None, "ep"),
    )
    out_specs = (P("pipe", "ep", None), P("pipe", "ep", None))
    return jax.shard_map(body, mesh=mesh, in_specs=in_specs, out_specs=out_specs, check_vma=False)
```
